32 devices in a mesh: grp: 2 (over x), area: 8 (over z, y), ctg: 2 (over core).
Axes of the slice: x: 2, y: 2, z: 4, core: 2. Of those that a mesh axis runs over, the one named last changes fastest.
Arguments:
- area_size: int32 [16], P(('grp', 'area')), parts along dimension 0, may hold values from 299 to 1024, as said below
- tie_peer: int32 [16, 42], P(('grp', 'area')), parts along dimension 0, may hold values from 0 to 7, as said below
- kkt_diag: float32 [16, 2, 1024], P(('grp', 'area'), 'ctg'), parts along dimension 0, may hold values from 0.5 to 1
- kkt_offdiag: float32 [16, 2, 1024, 1024], P(('grp', 'area'), 'ctg'), parts along dimension 0, may hold values from -0.1875 to 0.1875
- cost: float32 [16, 2, 1024, 256], P(('grp', 'area'), 'ctg'), parts along dimension 0, may hold values from -6 to 6
- consensus: float32 [16, 2, 1024, 256], P(('grp', 'area'), 'ctg'), parts along dimension 0, may hold values from -4 to 4
- dual: float32 [16, 2, 1024, 256], P(('grp', 'area'), 'ctg'), parts along dimension 0, may hold values from -4 to 4
- limit: float32 [16, 1024, 256], P(('grp', 'area')), parts along dimension 0, may hold values from 0.3 to 1.5
Outputs:
- agreed_out: float32 [16, 2, 1024, 256], P(('grp', 'area'), 'ctg'), parts along dimension 0
- dual_out: float32 [16, 2, 1024, 256], P(('grp', 'area'), 'ctg'), parts along dimension 0
The draws below stay inside these ranges and needn't reach their ends.
There are 2 independent parts, one for each index of `grp`. The reference program is written for one: setup_inputs(seed, part) draws one part's arguments, and reference() takes and returns one part's arrays. A program takes and returns all parts, laid end to end along the dimension named above; each array names one. Nothing has to cross between parts.
Inputs may be any that keep to these rules, and one draw needn't show every extreme that they name: `area_size`: some area has exactly 1024 live slots. `tie_peer`: never the area itself; each area has exactly 6 tie slots to each other area.
All inputs are finite; a program needn't handle non-finite values.
Results may differ from the reference program's by a relative error of at most 0.0003.
Values sent between devices are 32-bit elements; how exact they have to be, the bound alone decides.
No kernel may reach another device: no remote copies, remote signals or barrier semaphores. Data moves between devices by JAX's collectives and lax.ppermute only.
A program may use at most 64 MiB of HBM per device.

```python
import math
import jax
import jax.numpy as jnp
from jax import lax

SLOTS = 1024
HOURS = 256
GENS = 256
TIE_PAIR = 6
ITERS = 3
N_AREA = 8
N_CTG = 2


def draw_area_size(key, part):
    first, second = jax.random.split(jax.random.fold_in(key, 11))
    lowest = GENS + TIE_PAIR * (N_AREA - 1) + 1
    sizes = jax.random.randint(first, (N_AREA,), lowest, SLOTS + 1)
    chosen = jax.random.randint(second, (), 0, N_AREA)
    return sizes.at[chosen].set(SLOTS).astype(jnp.int32)


def draw_tie_peer(key, part):
    ties = TIE_PAIR * (N_AREA - 1)
    subkeys = jax.random.split(jax.random.fold_in(key, 23), N_AREA)
    shuffled = jax.vmap(lambda single: jax.random.permutation(single, ties))(subkeys)
    areas = jnp.arange(N_AREA)[:, None]
    return ((areas + 1 + shuffled // TIE_PAIR) % N_AREA).astype(jnp.int32)


def level_of(key, shape, shards, least, high):
    def one(position, parts):
        heights = jax.random.uniform(jax.random.fold_in(jax.random.fold_in(key, 6), position), (parts,), jnp.float32, least / len(shards), high / len(shards))
        return jnp.repeat(jnp.exp(heights), shape[position] // parts).reshape((-1,) + (1,) * (len(shape) - position - 1))

    level = one(*shards[0])
    for cut in shards[1:]:
        level = level * one(*cut)
    return level


def centred(own_key, extent, deviation, most, shards=(), kind=jnp.bfloat16):
    values = deviation * jax.random.normal(own_key, extent, jnp.float32)
    if shards:
        values = values * level_of(own_key, extent, shards, -0.22, 0.18)
    return jnp.clip(values, -most, most).astype(kind)


def setup_inputs(seed: int = 0, part: int = 0) -> dict:
    arg_keys = jax.random.split(jax.random.key(seed), 9)
    part_keys = jax.random.split(jax.random.fold_in(arg_keys[8], part), 9)
    area_size = draw_area_size(jax.random.fold_in(jax.random.fold_in(arg_keys[8], part), 71), part)
    tie_peer = draw_tie_peer(jax.random.fold_in(jax.random.fold_in(arg_keys[8], part), 71), part)
    kkt_diag = jnp.clip(0.5 + 0.5 * jax.random.uniform(part_keys[2], (N_AREA, N_CTG, SLOTS), jnp.float32) ** level_of(part_keys[2], (N_AREA, N_CTG, SLOTS), ((0, 8), (1, 2)), -0.2, 0.2), 0.5, 1.0)
    kkt_offdiag = centred(part_keys[3], (N_AREA, N_CTG, SLOTS, SLOTS), SLOTS ** -0.5, 0.1875, ((0, 8), (1, 2)), jnp.float32)
    cost = centred(part_keys[4], (N_AREA, N_CTG, SLOTS, HOURS), 1.0, 6.0, ((0, 8), (1, 2)), jnp.float32)
    consensus = centred(part_keys[5], (N_AREA, N_CTG, SLOTS, HOURS), 0.5, 4.0, ((0, 8), (1, 2)), jnp.float32)
    dual = centred(part_keys[6], (N_AREA, N_CTG, SLOTS, HOURS), 0.5, 4.0, ((0, 8), (1, 2)), jnp.float32)
    limit = jnp.clip(jnp.exp(math.log(1.5) - 1.60943787 * jax.random.uniform(part_keys[7], (N_AREA, SLOTS, HOURS), jnp.float32) ** level_of(part_keys[7], (N_AREA, SLOTS, HOURS), ((0, 8),), -0.2, 0.2)), 0.3, 1.5)
    return dict(area_size=area_size, tie_peer=tie_peer, kkt_diag=kkt_diag, kkt_offdiag=kkt_offdiag, cost=cost, consensus=consensus, dual=dual, limit=limit)


def tie_dest(peers):
    count = peers.shape[0]
    order = jnp.arange(count)
    same = (peers[:, None] == peers[None, :]) & (order[:, None] < order[None, :])
    rank = jnp.sum(same.astype(jnp.int32), axis=0)
    return (peers * TIE_PAIR + rank).astype(jnp.int32)


def reference(area_size, tie_peer, kkt_diag, kkt_offdiag, cost, consensus, dual, limit):
    ties = TIE_PAIR * (N_AREA - 1)
    live = (jnp.arange(SLOTS)[None, :] < area_size[:, None]).astype(jnp.float32)[:, None, :, None]
    dest = jax.vmap(tie_dest)(tie_peer)
    bound = limit[:, None]
    agreed = consensus
    dual_var = dual

    def product(pieces):
        return jnp.einsum("cij,cjh->cih", pieces[0], pieces[1], precision=lax.Precision.HIGHEST)

    def scatter_one(values, where):
        return jnp.zeros((N_CTG, N_AREA * TIE_PAIR, HOURS), jnp.float32).at[:, where].set(values)

    def take_one(values, where):
        return values[:, where]

    for iteration in range(ITERS):
        right_side = live * (agreed - dual_var - cost)
        applied = lax.map(product, (kkt_offdiag, right_side))
        primal = live * (kkt_diag[..., None] * right_side + applied)
        shifted = primal + dual_var
        gen_mean = jnp.broadcast_to(jnp.mean(shifted[:, :, :GENS], axis=1, keepdims=True), (N_AREA, N_CTG, GENS, HOURS))
        tie_part = shifted[:, :, GENS:GENS + ties]
        sent = jax.vmap(scatter_one)(tie_part, dest)
        sent = sent.reshape(N_AREA, N_CTG, N_AREA, TIE_PAIR, HOURS)
        got = jnp.transpose(sent, (2, 1, 0, 3, 4)).reshape(N_AREA, N_CTG, N_AREA * TIE_PAIR, HOURS)
        other = jax.vmap(take_one)(got, dest)
        averaged = jnp.concatenate([gen_mean, 0.5 * (tie_part + other), shifted[:, :, GENS + ties:]], axis=2)
        agreed = live * jnp.clip(averaged, -bound, bound)
        dual_var = live * (dual_var + primal - agreed)
    return agreed, dual_var
```

```python
import jax
import jax.numpy as jnp
from jax import lax
from jax.sharding import PartitionSpec as P

GENS = 256
ITERS = 3


def tie_dest(peers, pair_lines):
    count = peers.shape[0]
    order = jnp.arange(count)
    same = (peers[:, None] == peers[None, :]) & (order[:, None] < order[None, :])
    rank = jnp.sum(same.astype(jnp.int32), axis=0)
    return peers * pair_lines + rank


def apply_rows(matrix, right_side):
    return jnp.dot(
        matrix, right_side, precision=lax.Precision.HIGH, preferred_element_type=jnp.float32
    )


def mean_over_ctg(values, scenarios):
    total = values
    for step in range(1, scenarios):
        pairs = [(i, (i + step) % scenarios) for i in range(scenarios)]
        total = total + lax.ppermute(values, "ctg", pairs)
    return total / scenarios


def local(area_size, tie_peer, kkt_diag, kkt_offdiag, cost, consensus, dual, limit):
    areas = lax.axis_size("area")
    scenarios = lax.axis_size("ctg")
    peers = tie_peer[0]
    ties = peers.shape[0]
    pair_lines = ties // (areas - 1)
    dest = tie_dest(peers, pair_lines)
    slots = cost.shape[2]
    hours = cost.shape[3]
    shared = GENS + ties
    live = (jnp.arange(slots) < area_size[0]).astype(jnp.float32)[:, None]
    offdiag = kkt_offdiag[0, 0]
    diagonal = kkt_diag[0, 0][:, None]
    bound = limit[0]
    linear = cost[0, 0]
    agreed = consensus[0, 0]
    dual_var = dual[0, 0]
    spread = (dest[None, :] == jnp.arange(areas * pair_lines)[:, None]).astype(jnp.float32)
    for iteration in range(ITERS):
        right_side = live * (agreed - dual_var - linear)
        primal = live * (diagonal * right_side + apply_rows(offdiag, right_side))
        shifted = primal + dual_var
        tie_part = shifted[GENS:shared]
        sent = jnp.dot(spread, tie_part, precision=lax.Precision.HIGHEST)
        got = lax.all_to_all(
            sent.reshape(areas, pair_lines, hours), "area", split_axis=0, concat_axis=0, tiled=True
        ).reshape(areas * pair_lines, hours)
        gen_mean = mean_over_ctg(shifted[:GENS], scenarios)
        other = jnp.dot(spread.T, got, precision=lax.Precision.HIGHEST)
        averaged = jnp.concatenate([gen_mean, 0.5 * (tie_part + other), shifted[shared:]], axis=0)
        agreed = live * jnp.clip(averaged, -bound, bound)
        dual_var = live * (dual_var + primal - agreed)
    return (agreed[None, None], dual_var[None, None])


def solution(mesh):
    return jax.shard_map(
        local,
        mesh=mesh,
        in_specs=(
            P(("grp", "area")),
            P(("grp", "area"), None),
            P(("grp", "area"), "ctg", None),
            P(("grp", "area"), "ctg", None, None),
            P(("grp", "area"), "ctg", None, None),
            P(("grp", "area"), "ctg", None, None),
            P(("grp", "area"), "ctg", None, None),
            P(("grp", "area"), None, None),
        ),
        out_specs=(P(("grp", "area"), "ctg", None, None), P(("grp", "area"), "ctg", None, None)),
        check_vma=False,
    )
```
